32 devices in a mesh: dp: 8 (over y, x, core), mp: 4 (over z).
Axes of the slice: x: 2, y: 2, z: 4, core: 2. Of those that a mesh axis runs over, the one named last changes fastest.
Arguments:
- tokens: bfloat16 [2, 8, 512, 2048], P(None, 'dp', 'mp'), may hold values from -6 to 6
- segments: int32 [2, 8, 512], P(None, 'dp', 'mp'), may hold values from 0 to 2, never falling along the last dimension, each value on 1 to 400 neighbouring positions
- query_weight: bfloat16 [2048, 2048], P('dp', 'mp'), may hold values from -0.125 to 0.125
- key_weight: bfloat16 [2048, 2048], P('dp', 'mp'), may hold values from -0.125 to 0.125
- value_weight: bfloat16 [2048, 4096], P('dp', 'mp'), may hold values from -0.125 to 0.125
- gate_weight: bfloat16 [2048, 4096], P('dp', 'mp'), may hold values from -0.125 to 0.125
- out_weight: bfloat16 [2048, 4096], P('dp', 'mp'), may hold values from -0.09375 to 0.09375
- up_weight: bfloat16 [2048, 4096], P('dp', 'mp'), may hold values from -0.125 to 0.125
- down_weight: bfloat16 [2048, 4096], P('dp', 'mp'), may hold values from -0.09375 to 0.09375
- gain_before: bfloat16 [2048], P('dp'), may hold values from 0.099609375 to 1.8984375
- bias_before: bfloat16 [2048], P('dp'), may hold values from -3 to 3
- gain_middle: bfloat16 [2048], P('dp'), may hold values from 0.099609375 to 1.8984375
- bias_middle: bfloat16 [2048], P('dp'), may hold values from -3 to 3
- cotangent: bfloat16 [2, 8, 512, 2048], P(None, 'dp', 'mp'), may hold values from -6 to 6
Outputs:
- block_out: bfloat16 [2, 8, 512, 2048], P(None, 'dp', 'mp')
- tokens_grad: bfloat16 [2, 8, 512, 2048], P(None, 'dp', 'mp')
- query_grad: float32 [2048, 2048], P('dp', 'mp')
- key_grad: float32 [2048, 2048], P('dp', 'mp')
- value_grad: float32 [2048, 4096], P('dp', 'mp')
- gate_grad: float32 [2048, 4096], P('dp', 'mp')
- out_grad: float32 [2048, 4096], P('dp', 'mp')
- up_grad: float32 [2048, 4096], P('dp', 'mp')
- down_grad: float32 [2048, 4096], P('dp', 'mp')
- norm_grads: float32 [4, 2048], P(None, 'dp')
The draws below stay inside these ranges and needn't reach their ends.
Inputs may be any that keep to these rules, and one draw needn't show every extreme that they name: `segments`: within each sequence the numbers start at 0, never fall and rise by 1 at each document boundary; each of the 3 documents spans 1 to 400 positions, and one spans exactly 400.
All inputs are finite; a program needn't handle non-finite values.
Results may differ from the reference program's by a relative error of at most 0.02.
Values may be sent and summed in bfloat16 or wider, within the bound.
No kernel may reach another device: no remote copies, remote signals or barrier semaphores. Data moves between devices by JAX's collectives and lax.ppermute only.
A program may use at most 192 MiB of HBM per device.

```python
import math
import jax
import jax.numpy as jnp
import numpy as np
from jax import lax

D = 2048
H = 8
DK = 256
DV = 512
FF = 4096
SEQ_LEN = 512
MICRO = 2
DOCS = 3
DOC_MOST = 400
NSEQ = 8
N_MP = 4


def raised(entries, key, source, target, shards_of, factor):
    def block_of(position):
        return (jnp.arange(entries.shape[position]) // (entries.shape[position] // shards_of)).reshape((-1,) + (1,) * (entries.ndim - 1 - position))

    near = jax.random.permutation(key, shards_of)[block_of(target)]
    other_side = (block_of(target) + shards_of // 2) % shards_of
    return jnp.where((block_of(source) == near) | (block_of(source) == other_side), factor * entries, entries)


def steps_of(stream_key, extent, shards, least, high):
    level = 1.0
    for position, blocks in shards:
        draws = jax.random.uniform(jax.random.fold_in(jax.random.fold_in(stream_key, 6), position), (blocks,), jnp.float32, least / len(shards), high / len(shards))
        level = level * jnp.repeat(jnp.exp(draws), extent[position] // blocks).reshape((-1,) + (1,) * (len(extent) - 1 - position))
    return level


def split_up(number_of, total, bound, slope):
    loads = [(1 << 20) // math.isqrt(standing ** slope) + 1 for standing in range(2, number_of + 1)]
    surplus, counts = total - bound - (number_of - 1), [1] * (number_of - 1)
    while surplus > 0:
        movable = [i for i in range(number_of - 1) if counts[i] < bound]
        pool, budget = sum([loads[i] for i in movable]), surplus
        for i in movable:
            addition = min(bound - counts[i], max(1, budget * loads[i] // pool), surplus)
            counts[i] = counts[i] + addition
            surplus = surplus - addition
    return np.array([bound] + counts)


def ragged(stream_key, count, total, most, lean):
    if count == 2:
        one = jax.random.randint(stream_key, (), max(1, total - most), min(most, total - 1) + 1)
        return jnp.stack([one, total - one])
    lengths = jnp.asarray(split_up(count, total, most, lean), jnp.int32)
    couples = (count - 1) // 2
    giver, receiver = lengths[1:1 + 2 * couples:2], lengths[2:2 + 2 * couples:2]
    slack = jnp.minimum(giver - 1, most - receiver)
    shifted = jax.random.randint(jax.random.fold_in(stream_key, 1), (couples,), 0, 1 << 20) % (slack + 1)
    lengths = lengths.at[1:1 + 2 * couples:2].set(giver - shifted).at[2:2 + 2 * couples:2].set(receiver + shifted)
    return lengths[jax.random.permutation(jax.random.fold_in(stream_key, 2), count)]


def bell_draw(own_key, shape, deviation, reach, split=(), kind=jnp.bfloat16):
    loudness = steps_of(own_key, shape, split, -0.22, 0.18) if split else 1.0
    entries = jax.random.normal(own_key, shape, jnp.float32) * deviation * loudness
    return jnp.minimum(jnp.maximum(entries, -reach), reach).astype(kind)


def bell_draw_with(stream_key, shape, scale, reach, split, heavy, kind=jnp.bfloat16):
    result = scale * jax.random.normal(stream_key, shape, jnp.float32)
    if split:
        result = result * steps_of(stream_key, shape, split, -0.22, 0.18)
    return jnp.clip(raised(result, jax.random.fold_in(stream_key, 3), *heavy), -reach, reach).astype(kind)


def setup_inputs(seed: int = 0) -> dict:
    streams_of = jax.random.split(jax.random.key(seed), 15)
    tokens = bell_draw(streams_of[0], (MICRO, NSEQ, SEQ_LEN, D), 1.0, 6.0, ((1, 8), (2, 4)))
    segments = jax.vmap(lambda own: jnp.searchsorted(jnp.cumsum(ragged(own, DOCS, SEQ_LEN, DOC_MOST, 0)), jnp.arange(SEQ_LEN), side="right"))(jax.random.split(streams_of[1], MICRO * NSEQ)).reshape((MICRO, NSEQ, SEQ_LEN)).astype(jnp.int32)
    query_weight = bell_draw(streams_of[2], (D, H * DK), D ** -0.5, 0.125, ((0, 8), (1, 4)))
    key_weight = bell_draw(streams_of[3], (D, H * DK), D ** -0.5, 0.125, ((0, 8), (1, 4)))
    value_weight = bell_draw(streams_of[4], (D, H * DV), D ** -0.5, 0.125, ((0, 8), (1, 4)))
    gate_weight = bell_draw(streams_of[5], (D, H * DV), D ** -0.5, 0.125, ((0, 8), (1, 4)))
    out_weight = bell_draw(streams_of[6], (D, H * DV), (H * DV) ** -0.5, 0.09375, ((0, 8), (1, 4)))
    up_weight = bell_draw(streams_of[7], (D, FF), D ** -0.5, 0.125, ((0, 8), (1, 4)))
    down_weight = bell_draw(streams_of[8], (D, FF), FF ** -0.5, 0.09375, ((0, 8), (1, 4)))
    gain_before = jnp.clip(1.0 + 0.18 * jax.random.normal(streams_of[9], (D,), jnp.float32), 0.099609375, 1.8984375).astype(jnp.bfloat16)
    bias_before = bell_draw(streams_of[10], (D,), 0.5, 3.0, ((0, 8),))
    gain_middle = jnp.clip(1.0 + 0.18 * jax.random.normal(streams_of[11], (D,), jnp.float32), 0.099609375, 1.8984375).astype(jnp.bfloat16)
    bias_middle = bell_draw(streams_of[12], (D,), 0.5, 3.0, ((0, 8),))
    cotangent = bell_draw_with(streams_of[13], (MICRO, NSEQ, SEQ_LEN, D), 1.0, 6.0, ((1, 8), (2, 4)), (1, 3, 8, 2.0))
    return dict(tokens=tokens, segments=segments, query_weight=query_weight, key_weight=key_weight, value_weight=value_weight, gate_weight=gate_weight, out_weight=out_weight, up_weight=up_weight, down_weight=down_weight, gain_before=gain_before, bias_before=bias_before, gain_middle=gain_middle, bias_middle=bias_middle, cotangent=cotangent)


EPS = 1e-05
GROUP_EPS = 1.0
ROOT_HALF = 0.7071067811865476
INV_ROOT_TWO_PI = 0.3989422804014327

def layer_norm(values, gain_vec, bias_vec, epsilon=EPS):
    average = lax.optimization_barrier(jnp.mean(values, axis=-1, keepdims=True))
    centred = values - average
    inv_std = lax.rsqrt(lax.optimization_barrier(jnp.mean(centred * centred, axis=-1, keepdims=True)) + epsilon)
    scaled = centred * inv_std
    return (scaled * gain_vec + bias_vec, scaled, inv_std)

def norm_back(grad_in, gain_vec, scaled, inv_std):
    scaled_grad = grad_in * gain_vec
    return inv_std * (scaled_grad - lax.optimization_barrier(jnp.mean(scaled_grad, axis=-1, keepdims=True)) - scaled * lax.optimization_barrier(jnp.mean(scaled_grad * scaled, axis=-1, keepdims=True)))

def gelu_value(up_proj):
    return 0.5 * up_proj * (1.0 + lax.erf(up_proj * ROOT_HALF))

def gelu_slope(up_proj):
    return 0.5 * (1.0 + lax.erf(up_proj * ROOT_HALF)) + up_proj * jnp.exp(-0.5 * up_proj * up_proj) * INV_ROOT_TWO_PI

def decay_mask(seg_ids, decay_rates):
    seq_length = seg_ids.shape[0]
    positions = jnp.arange(seq_length, dtype=jnp.int32)
    lag_steps = positions[:, None] - positions[None, :]
    visible = (lag_steps >= 0) & (seg_ids[:, None] == seg_ids[None, :])
    lag_float = jnp.maximum(lag_steps, 0).astype(jnp.float32)
    decayed = jnp.exp(lag_float[None, :, :] * jnp.log(decay_rates)[:, None, None])
    return jnp.where(visible[None, :, :], decayed, jnp.float32(0.0))

def rotary_tables(seq_length, head_width):
    half_width = head_width // 2
    frequency = 10000.0 ** (-jnp.arange(half_width, dtype=jnp.float32) / half_width)
    angles = jnp.arange(seq_length, dtype=jnp.float32)[:, None] * frequency[None, :]
    return (jnp.cos(angles), jnp.sin(angles))

def rotate(field, cosine, sine_table, direction):
    half_width = field.shape[-1] // 2
    lower_half = field[..., :half_width]
    upper_half = field[..., half_width:]
    cos_b = cosine[:, None, :]
    sin_b = sine_table[:, None, :] * direction
    return jnp.concatenate([lower_half * cos_b - upper_half * sin_b, upper_half * cos_b + lower_half * sin_b], axis=-1)

def group_terms(left, right_rows):
    rows = left.shape[0]
    cols = left.shape[1]
    width = right_rows.shape[0]
    left_groups = left.astype(jnp.float32).reshape(rows, N_MP, cols // N_MP)
    right_groups = right_rows.astype(jnp.float32).reshape(width, N_MP, cols // N_MP)
    return jnp.einsum('rgc,dgc->grd', left_groups, right_groups)

def rounded_sum(partials):
    rounded = lax.optimization_barrier(partials.astype(jnp.bfloat16))
    return lax.optimization_barrier(jnp.sum(rounded.astype(jnp.float32), axis=0))

def reference(tokens, segments, query_weight, key_weight, value_weight, gate_weight, out_weight, up_weight, down_weight, gain_before, bias_before, gain_middle, bias_middle, cotangent):
    seq_length = tokens.shape[2]
    model_width = tokens.shape[3]
    cosine, sine_table = rotary_tables(seq_length, DK)
    decay_rates = 1.0 - 2.0 ** (-5.0 - jnp.arange(H).astype(jnp.float32))
    key_scale = DK ** (-0.5)

    def one_sequence(totals, seq_item):
        x_tokens, seg_ids, dy_tokens = seq_item
        x_float = x_tokens.astype(jnp.float32)
        norm_one, scaled_one, inv_one = layer_norm(x_float, gain_before, bias_before)
        normed = norm_one.astype(jnp.bfloat16)
        query_proj = jnp.dot(normed, query_weight, preferred_element_type=jnp.float32).reshape(seq_length, H, DK)
        key_proj = jnp.dot(normed, key_weight, preferred_element_type=jnp.float32).reshape(seq_length, H, DK)
        value_b = jnp.dot(normed, value_weight, preferred_element_type=jnp.float32).astype(jnp.bfloat16).reshape(seq_length, H, DV)
        gate_proj = jnp.dot(normed, gate_weight, preferred_element_type=jnp.float32)
        rotated_query_rows = rotate(query_proj, cosine, sine_table, 1.0).astype(jnp.bfloat16)
        rotated_key_rows = (rotate(key_proj, cosine, sine_table, 1.0) * key_scale).astype(jnp.bfloat16)
        head_decay_mask_stack = decay_mask(seg_ids, decay_rates)
        retention_score_matrix = jnp.einsum('beg,ieg->ebi', rotated_query_rows.astype(jnp.float32), rotated_key_rows.astype(jnp.float32)) * head_decay_mask_stack
        weights_b = retention_score_matrix.astype(jnp.bfloat16)
        retained = jnp.einsum('hnm,mhe->nhe', weights_b.astype(jnp.float32), value_b.astype(jnp.float32))
        plain_norm, grouped, group_inv = layer_norm(retained, 1.0, 0.0, GROUP_EPS)
        grouped_flat = grouped.reshape(seq_length, H * DV)
        gate_act = jax.nn.silu(gate_proj)
        gated = (gate_act * grouped_flat).astype(jnp.bfloat16)
        resid_mid = x_float + rounded_sum(group_terms(gated, out_weight))
        norm_two, scaled_two, inv_two = layer_norm(resid_mid, gain_middle, bias_middle)
        normed_two = norm_two.astype(jnp.bfloat16)
        up_proj = jnp.dot(normed_two, up_weight, preferred_element_type=jnp.float32)
        hidden = gelu_value(up_proj).astype(jnp.bfloat16)
        block_out = (resid_mid + rounded_sum(group_terms(hidden, down_weight))).astype(jnp.bfloat16)
        d_hidden = jnp.dot(dy_tokens, down_weight, preferred_element_type=jnp.float32)
        d_up = (d_hidden * gelu_slope(up_proj)).astype(jnp.bfloat16)
        down_part = jnp.dot(dy_tokens.T, hidden, preferred_element_type=jnp.float32)
        up_part = jnp.dot(normed_two.T, d_up, preferred_element_type=jnp.float32)
        d_normtwo = rounded_sum(group_terms(d_up, up_weight))
        d_resid = dy_tokens.astype(jnp.float32) + norm_back(d_normtwo, gain_middle, scaled_two, inv_two)
        d_resid_b = d_resid.astype(jnp.bfloat16)
        d_gated = jnp.dot(d_resid_b, out_weight, preferred_element_type=jnp.float32)
        out_part = jnp.dot(d_resid_b.T, gated, preferred_element_type=jnp.float32)
        gate_sig = jax.nn.sigmoid(gate_proj)
        d_gate = (d_gated * grouped_flat * gate_sig * (1.0 + gate_proj * (1.0 - gate_sig))).astype(jnp.bfloat16)
        d_grouped = (d_gated * gate_act).reshape(seq_length, H, DV)
        d_retained = norm_back(d_grouped, 1.0, grouped, group_inv).astype(jnp.bfloat16)
        retention_weight_gradient = (jnp.einsum('nhe,mhe->hnm', d_retained.astype(jnp.float32), value_b.astype(jnp.float32)) * head_decay_mask_stack).astype(jnp.bfloat16)
        d_value = jnp.einsum('hnm,nhe->mhe', weights_b.astype(jnp.float32), d_retained.astype(jnp.float32)).astype(jnp.bfloat16).reshape(seq_length, H * DV)
        rotated_query_gradient = jnp.einsum('lfg,gls->fls', retention_weight_gradient.astype(jnp.float32), rotated_key_rows.astype(jnp.float32))
        rotated_key_gradient = jnp.einsum('yjf,jyu->fyu', retention_weight_gradient.astype(jnp.float32), rotated_query_rows.astype(jnp.float32))
        d_query = rotate(rotated_query_gradient, cosine, sine_table, -1.0).astype(jnp.bfloat16).reshape(seq_length, H * DK)
        d_key = (rotate(rotated_key_gradient, cosine, sine_table, -1.0) * key_scale).astype(jnp.bfloat16).reshape(seq_length, H * DK)
        query_part = jnp.dot(normed.T, d_query, preferred_element_type=jnp.float32)
        key_part = jnp.dot(normed.T, d_key, preferred_element_type=jnp.float32)
        value_part = jnp.dot(normed.T, d_value, preferred_element_type=jnp.float32)
        gate_part = jnp.dot(normed.T, d_gate, preferred_element_type=jnp.float32)
        before_partials = group_terms(d_query, query_weight) + group_terms(d_key, key_weight) + group_terms(d_value, value_weight) + group_terms(d_gate, gate_weight)
        d_normone = rounded_sum(before_partials)
        tokens_grad = (d_resid + norm_back(d_normone, gain_before, scaled_one, inv_one)).astype(jnp.bfloat16)
        norm_part = jnp.stack([lax.optimization_barrier(jnp.sum(d_normone * scaled_one, axis=0)), lax.optimization_barrier(jnp.sum(d_normone, axis=0)), lax.optimization_barrier(jnp.sum(d_normtwo * scaled_two, axis=0)), lax.optimization_barrier(jnp.sum(d_normtwo, axis=0))])
        parts = (query_part, key_part, value_part, gate_part, out_part, up_part, down_part, norm_part)
        new_totals = tuple((total + part for total, part in zip(totals, parts)))
        return (new_totals, (block_out, tokens_grad))
    initial = (jnp.zeros((model_width, H * DK), jnp.float32), jnp.zeros((model_width, H * DK), jnp.float32), jnp.zeros((model_width, H * DV), jnp.float32), jnp.zeros((model_width, H * DV), jnp.float32), jnp.zeros((model_width, H * DV), jnp.float32), jnp.zeros((model_width, FF), jnp.float32), jnp.zeros((model_width, FF), jnp.float32), jnp.zeros((4, model_width), jnp.float32))
    seq_items = (tokens.reshape(-1, seq_length, model_width), segments.reshape(-1, seq_length), cotangent.reshape(-1, seq_length, model_width))
    totals, stacked = lax.scan(one_sequence, initial, seq_items)
    block_out = stacked[0].reshape(tokens.shape)
    tokens_grad = stacked[1].reshape(tokens.shape)
    return (block_out, tokens_grad, totals[0], totals[1], totals[2], totals[3], totals[4], totals[5], totals[6], totals[7])
```

```python
import functools

import jax
import jax.numpy as jnp
from jax import lax
from jax.experimental import pallas as pl
from jax.experimental.pallas import tpu as pltpu
from jax.sharding import PartitionSpec as P

DK = 256
DV = 512

EPS = 1e-05
GROUP_EPS = 1.0
ROOT_HALF = 0.7071067811865476
INV_ROOT_TWO_PI = 0.3989422804014327

F32 = jnp.float32
BF16 = jnp.bfloat16


def layer_norm(values, gain_vec, bias_vec, epsilon=EPS):
    average = jnp.mean(values, axis=-1, keepdims=True)
    centred = values - average
    inv_std = lax.rsqrt(jnp.mean(centred * centred, axis=-1, keepdims=True) + epsilon)
    scaled = centred * inv_std
    return (scaled * gain_vec + bias_vec, scaled, inv_std)


def norm_back(grad_in, gain_vec, scaled, inv_std):
    scaled_grad = grad_in * gain_vec
    return inv_std * (
        scaled_grad
        - jnp.mean(scaled_grad, axis=-1, keepdims=True)
        - scaled * jnp.mean(scaled_grad * scaled, axis=-1, keepdims=True)
    )


def gelu_value(up_proj):
    return 0.5 * up_proj * (1.0 + lax.erf(up_proj * ROOT_HALF))


def gelu_slope(up_proj):
    return (
        0.5 * (1.0 + lax.erf(up_proj * ROOT_HALF))
        + up_proj * jnp.exp(-0.5 * up_proj * up_proj) * INV_ROOT_TWO_PI
    )


def decay_mask(seg_ids, decay_rate):
    seq_length = seg_ids.shape[0]
    positions = jnp.arange(seq_length, dtype=jnp.int32)
    lag_steps = positions[:, None] - positions[None, :]
    visible = (lag_steps >= 0) & (seg_ids[:, None] == seg_ids[None, :])
    lag_float = jnp.maximum(lag_steps, 0).astype(F32)
    return jnp.where(visible, jnp.exp(lag_float * jnp.log(decay_rate)), F32(0.0))


def rotary_tables(seq_length, head_width):
    half_width = head_width // 2
    frequency = 10000.0 ** (-jnp.arange(half_width, dtype=F32) / half_width)
    angles = jnp.arange(seq_length, dtype=F32)[:, None] * frequency[None, :]
    return (jnp.cos(angles), jnp.sin(angles))


def rotate(head, cosine, sine):
    half_width = head.shape[-1] // 2
    lower = head[:, :half_width]
    upper = head[:, half_width:]
    return jnp.concatenate([lower * cosine - upper * sine, upper * cosine + lower * sine], axis=-1)


def dot(left, right, left_axis=1, right_axis=0):
    return lax.dot_general(
        left, right, (((left_axis,), (right_axis,)), ((), ())), preferred_element_type=F32
    )


class Plane:
    def __init__(self, size):
        self.size = size
        self.chips = [1 << bit for bit in range(1, size.bit_length() - 1)]
        self.masks = [0]
        for mask in self.chips:
            self.masks = self.masks + [held ^ mask for held in self.masks]

    def swap(self, value, mask):
        return lax.ppermute(value, "dp", [(i, i ^ mask) for i in range(self.size)])

    def gather_chips(self, block, chips):
        if not chips:
            return [block]
        if len(chips) == 2:
            first, second = chips
            one = self.swap(block, first)
            two = self.swap(block, second)
            half = block.shape[0] // 2
            both = jnp.concatenate([self.swap(one[:half], second), self.swap(two[half:], first)])
            return [block, one, two, both]
        held = self.gather_chips(block, chips[:-1])
        other = self.swap(jnp.concatenate(held), chips[-1])
        return held + jnp.split(other, len(held))

    def gather(self, block):
        near = jnp.concatenate(self.gather_chips(block, self.chips))
        return near, self.swap(near, 1)

    def scatter_chips(self, parts, chips):
        if not chips:
            return parts[0]
        if len(chips) == 2:
            first, second = chips
            own, one, two, both = parts
            half = own.shape[0] // 2
            from_two = self.swap(both[:half].astype(BF16), second)
            from_one = self.swap(both[half:].astype(BF16), first)
            one = jnp.concatenate([one[:half] + from_two, one[half:]]).astype(BF16)
            two = jnp.concatenate([two[:half], two[half:] + from_one]).astype(BF16)
            return own + self.swap(one, first) + self.swap(two, second)
        count = len(parts) // 2
        far = self.swap(jnp.concatenate(parts[count:]).astype(BF16), chips[-1])
        merged = [part + got for part, got in zip(parts[:count], jnp.split(far, count))]
        return self.scatter_chips(merged, chips[:-1])

    def scatter(self, near, far):
        merged = near + self.swap(far.astype(BF16), 1).astype(F32)
        return self.scatter_chips(jnp.split(merged, len(self.masks)), self.chips)

    def place(self, near, far, index):
        count = len(self.masks)
        rows = near.shape[0] // count
        cols = near.shape[1]
        table = jnp.array(self.masks + [mask ^ 1 for mask in self.masks], jnp.int32) ^ index

        def kernel(table_ref, near_ref, far_ref, out_ref):
            step = pl.program_id(0)

            @pl.when(step < count)
            def _():
                out_ref[...] = near_ref[...]

            @pl.when(step >= count)
            def _():
                out_ref[...] = far_ref[...]

        return pl.pallas_call(
            kernel,
            out_shape=jax.ShapeDtypeStruct((2 * count * rows, cols), near.dtype),
            grid_spec=pltpu.PrefetchScalarGridSpec(
                num_scalar_prefetch=1,
                grid=(2 * count,),
                in_specs=[
                    pl.BlockSpec((rows, cols), lambda r, t: (jnp.minimum(r, count - 1), 0)),
                    pl.BlockSpec((rows, cols), lambda r, t: (jnp.maximum(r - count, 0), 0)),
                ],
                out_specs=pl.BlockSpec((rows, cols), lambda r, t: (t[r], 0)),
            ),
            cost_estimate=pl.CostEstimate(
                flops=0, transcendentals=0, bytes_accessed=8 * count * rows * cols
            ),
        )(table, near, far)

    def pick(self, whole, index):
        blocks = whole.reshape(self.size, whole.shape[0] // self.size, whole.shape[1])
        near = [lax.dynamic_index_in_dim(blocks, index ^ m, 0, False) for m in self.masks]
        far = [lax.dynamic_index_in_dim(blocks, index ^ m ^ 1, 0, False) for m in self.masks]
        return jnp.concatenate(near), jnp.concatenate(far)


def body(
    dp_size,
    tokens,
    segments,
    query_weight,
    key_weight,
    value_weight,
    gate_weight,
    out_weight,
    up_weight,
    down_weight,
    gain_before,
    bias_before,
    gain_middle,
    bias_middle,
    cotangent,
):
    plane = Plane(dp_size)
    index = lax.axis_index("dp")
    micro_count, seq_count, local_length, model_width = tokens.shape
    heads_here = query_weight.shape[1] // DK
    qk_cols = heads_here * DK
    hidden_share = up_weight.shape[1] // dp_size
    micro = range(micro_count)
    key_scale = DK ** (-0.5)

    shares = (
        jnp.concatenate([query_weight, key_weight], axis=1),
        value_weight,
        gate_weight,
        out_weight,
    )
    sides = [plane.gather(share) for share in shares]
    qk_full, value_full, gate_full, out_full = [
        plane.place(near, far, index) for near, far in sides
    ]
    norm_stack = lax.all_gather(
        jnp.stack([gain_before, bias_before, gain_middle, bias_middle]), "dp", axis=1, tiled=True
    ).astype(F32)
    gain_one, bias_one, gain_two, bias_two = [norm_stack[i] for i in range(4)]

    seg_full = lax.all_gather(segments, "mp", axis=2, tiled=True)
    seq_length = seg_full.shape[2]
    row_count = seq_count * seq_length
    local_rows = seq_count * local_length
    tokens_full = [
        lax.all_gather(tokens[b], "mp", axis=1, tiled=True).reshape(row_count, model_width)
        for b in micro
    ]
    x_local = [tokens[b].reshape(local_rows, model_width).astype(F32) for b in micro]
    dy_local = [cotangent[b].reshape(local_rows, model_width) for b in micro]

    ffn_share = jnp.concatenate(
        [
            up_weight.reshape(-1, dp_size, hidden_share),
            down_weight.reshape(-1, dp_size, hidden_share),
        ],
        axis=2,
    ).reshape(-1, 2 * dp_size * hidden_share)
    ffn_share = lax.all_to_all(ffn_share, "dp", 1, 0, tiled=True)
    ffn_all = lax.all_gather(ffn_share, "mp", axis=0)
    mp_size = ffn_all.shape[0]
    hidden_here = mp_size * hidden_share
    up_full = ffn_all[:, :, :hidden_share].transpose(1, 0, 2).reshape(model_width, hidden_here)
    down_full = ffn_all[:, :, hidden_share:].transpose(1, 0, 2).reshape(model_width, hidden_here)

    head_ids = lax.axis_index("mp") * heads_here + jnp.arange(heads_here, dtype=jnp.int32)
    decay_rates = 1.0 - 2.0 ** (-5.0 - head_ids.astype(F32))
    cosine, sine = rotary_tables(seq_length, DK)

    def to_owner(terms):
        return lax.psum_scatter(
            terms.astype(BF16).reshape(seq_count, seq_length, model_width),
            "mp",
            scatter_dimension=1,
            tiled=True,
        ).reshape(local_rows, model_width).astype(F32)

    def to_group(rows):
        return lax.all_gather(
            rows.reshape(seq_count, local_length, model_width), "mp", axis=1, tiled=True
        ).reshape(row_count, model_width)

    saved = []
    resid = []
    for b in micro:
        x_full = tokens_full[b].astype(F32)
        norm_full, scaled_full, _ = layer_norm(x_full, gain_one, bias_one)
        normed = norm_full.astype(BF16)
        qk = dot(normed, qk_full)
        value_b = dot(normed, value_full).astype(BF16)
        gate = dot(normed, gate_full)
        grouped_cols = []
        heads = []
        for s in range(seq_count):
            rows = slice(s * seq_length, (s + 1) * seq_length)
            row_cols = []
            for h in range(heads_here):
                mask = decay_mask(seg_full[b, s], decay_rates[h])
                q_head = rotate(qk[rows, h * DK : (h + 1) * DK], cosine, sine).astype(BF16)
                k_cols = slice(qk_cols + h * DK, qk_cols + (h + 1) * DK)
                k_head = (rotate(qk[rows, k_cols], cosine, sine) * key_scale).astype(BF16)
                v_head = value_b[rows, h * DV : (h + 1) * DV]
                weights = (dot(q_head, k_head, 1, 1) * mask).astype(BF16)
                _, grouped, group_inv = layer_norm(dot(weights, v_head), 1.0, 0.0, GROUP_EPS)
                row_cols.append(grouped)
                heads.append((q_head, k_head, v_head, weights, mask, grouped, group_inv))
            grouped_cols.append(jnp.concatenate(row_cols, axis=1))
        grouped_flat = jnp.concatenate(grouped_cols)
        gated = (jax.nn.silu(gate) * grouped_flat).astype(BF16)
        mix = to_owner(dot(gated, out_full, 1, 1))
        saved.append((normed, scaled_full, gate, heads, grouped_flat, gated))
        resid.append(x_local[b] + mix)

    outs = []
    middle = []
    for b in micro:
        norm_two, scaled_two, inv_two = layer_norm(resid[b], gain_two, bias_two)
        rows_two = plane.gather(norm_two.astype(BF16))
        rows_dy = plane.gather(dy_local[b])
        ups = [dot(rows, up_full) for rows in rows_two]
        hiddens = [gelu_value(up).astype(BF16) for up in ups]
        terms = [dot(hidden, down_full, 1, 1) for hidden in hiddens]
        d_ups = [
            (dot(rows, down_full) * gelu_slope(up)).astype(BF16) for rows, up in zip(rows_dy, ups)
        ]
        d_terms = [dot(d_up, up_full, 1, 1) for d_up in d_ups]
        d_normtwo = plane.scatter(*d_terms)
        outs.append((resid[b] + plane.scatter(*terms)).astype(BF16))
        d_resid = dy_local[b].astype(F32) + norm_back(d_normtwo, gain_two, scaled_two, inv_two)
        middle.append((rows_two, rows_dy, hiddens, d_ups, d_normtwo, scaled_two, d_resid))

    up_part = sum(
        dot(rows, d_up, 0, 0) for m in middle for rows, d_up in zip(m[0], m[3])
    )
    down_part = sum(
        dot(rows, hidden, 0, 0) for m in middle for rows, hidden in zip(m[1], m[2])
    )
    ffn_part = jnp.stack([up_part, down_part], axis=0).astype(BF16)
    ffn_part = ffn_part.reshape(2, model_width, mp_size, hidden_share).transpose(2, 1, 0, 3)
    ffn_grad = lax.psum_scatter(
        ffn_part.reshape(mp_size, model_width, 2 * hidden_share),
        "mp",
        scatter_dimension=0,
        tiled=False,
    )
    ffn_grad = lax.all_to_all(ffn_grad, "dp", 0, 1, tiled=True)
    ffn_grad = ffn_grad.reshape(-1, dp_size, 2, hidden_share).astype(F32)
    up_grad = ffn_grad[:, :, 0].reshape(-1, dp_size * hidden_share)
    down_grad = ffn_grad[:, :, 1].reshape(-1, dp_size * hidden_share)

    token_grads = []
    norm_sums = 0.0
    parts = [0.0, 0.0, 0.0, 0.0]
    for b in micro:
        normed, scaled_full, gate, heads, grouped_flat, gated = saved[b]
        d_normtwo, scaled_two, d_resid = middle[b][4:]
        d_rows = to_group(d_resid.astype(BF16))
        d_gated = dot(d_rows, out_full)
        sig = jax.nn.sigmoid(gate)
        d_gate = (d_gated * grouped_flat * sig * (1.0 + gate * (1.0 - sig))).astype(BF16)
        d_grouped = d_gated * gate * sig
        dq_rows = []
        dv_rows = []
        at = iter(heads)
        for s in range(seq_count):
            rows = slice(s * seq_length, (s + 1) * seq_length)
            dq_cols, dk_cols, dv_cols = [], [], []
            for h in range(heads_here):
                q_head, k_head, v_head, weights, mask, grouped, group_inv = next(at)
                d_out = norm_back(
                    d_grouped[rows, h * DV : (h + 1) * DV], 1.0, grouped, group_inv
                ).astype(BF16)
                d_weights = (dot(d_out, v_head, 1, 1) * mask).astype(BF16)
                dv_cols.append(dot(weights, d_out, 0, 0).astype(BF16))
                dq_cols.append(rotate(dot(d_weights, k_head), cosine, -sine).astype(BF16))
                dk_cols.append(
                    (rotate(dot(d_weights, q_head, 0, 0), cosine, -sine) * key_scale).astype(BF16)
                )
            dq_rows.append(jnp.concatenate(dq_cols + dk_cols, axis=1))
            dv_rows.append(jnp.concatenate(dv_cols, axis=1))
        d_qk = jnp.concatenate(dq_rows)
        d_value = jnp.concatenate(dv_rows)
        before = (
            dot(d_qk, qk_full, 1, 1) + dot(d_value, value_full, 1, 1) + dot(d_gate, gate_full, 1, 1)
        )
        d_normone = to_owner(before)
        norm_sums = norm_sums + jnp.stack(
            [
                jnp.sum(before * scaled_full, axis=0),
                jnp.sum(before, axis=0),
                jnp.sum(d_normtwo * scaled_two, axis=0),
                jnp.sum(d_normtwo, axis=0),
            ]
        )
        _, scaled_one, inv_one = layer_norm(x_local[b], gain_one, bias_one)
        token_grads.append(
            (d_resid + norm_back(d_normone, gain_one, scaled_one, inv_one)).astype(BF16)
        )
        new = [
            dot(normed, d_qk, 0, 0),
            dot(normed, d_value, 0, 0),
            dot(normed, d_gate, 0, 0),
            dot(d_rows, gated, 0, 0),
        ]
        parts = [total + part for total, part in zip(parts, new)]
    qk_grad, value_grad, gate_grad, out_grad = [
        plane.scatter(*plane.pick(part, index)) for part in parts
    ]
    norm_sums = lax.psum(norm_sums, ("dp", "mp"))
    share = model_width // dp_size
    norm_grads = lax.dynamic_slice_in_dim(norm_sums, index * share, share, axis=1)

    local_shape = (seq_count, local_length, model_width)
    return (
        jnp.stack([out.reshape(local_shape) for out in outs]),
        jnp.stack([grad.reshape(local_shape) for grad in token_grads]),
        qk_grad[:, :qk_cols],
        qk_grad[:, qk_cols:],
        value_grad,
        gate_grad,
        out_grad,
        up_grad,
        down_grad,
        norm_grads,
    )


def solution(mesh):
    rows = P(None, "dp", "mp", None)
    weight = P("dp", "mp")
    vector = P("dp")
    in_specs = (rows, P(None, "dp", "mp")) + (weight,) * 7 + (vector,) * 4 + (rows,)
    out_specs = (rows, rows) + (weight,) * 7 + (P(None, "dp"),)
    return jax.shard_map(
        functools.partial(body, mesh.shape["dp"]),
        mesh=mesh,
        in_specs=in_specs,
        out_specs=out_specs,
        check_vma=False,
    )
```

```python
import functools

import jax
import jax.numpy as jnp
from jax import lax
from jax.experimental import pallas as pl
from jax.experimental.pallas import tpu as pltpu
from jax.sharding import PartitionSpec as P

DK = 256
DV = 512

EPS = 1e-05
GROUP_EPS = 1.0
ROOT_HALF = 0.7071067811865476
INV_ROOT_TWO_PI = 0.3989422804014327

F32 = jnp.float32
BF16 = jnp.bfloat16


def layer_norm(values, gain_vec, bias_vec, epsilon=EPS):
    average = jnp.mean(values, axis=-1, keepdims=True)
    centred = values - average
    inv_std = lax.rsqrt(jnp.mean(centred * centred, axis=-1, keepdims=True) + epsilon)
    scaled = centred * inv_std
    return (scaled * gain_vec + bias_vec, scaled, inv_std)


def norm_back(grad_in, gain_vec, scaled, inv_std):
    scaled_grad = grad_in * gain_vec
    return inv_std * (
        scaled_grad
        - jnp.mean(scaled_grad, axis=-1, keepdims=True)
        - scaled * jnp.mean(scaled_grad * scaled, axis=-1, keepdims=True)
    )


def rotary_tables(seq_length, head_width):
    half_width = head_width // 2
    frequency = 10000.0 ** (-jnp.arange(half_width, dtype=F32) / half_width)
    angles = jnp.arange(seq_length, dtype=F32)[:, None] * frequency[None, :]
    return (jnp.cos(angles), jnp.sin(angles))


def dot(left, right, left_axis=1, right_axis=0):
    return lax.dot_general(
        left, right, (((left_axis,), (right_axis,)), ((), ())), preferred_element_type=F32
    )


def tie(*values):
    return lax.optimization_barrier(values)


class Staged:
    def __init__(self, steps):
        self.steps = steps
        self.value = next(steps)

    def ahead_of(self, *others):
        count = len(self.value)
        tied = tie(*self.value, *others)
        self.value = tied[:count]
        self.step()
        return tied[count:]

    def step(self):
        try:
            self.value = self.steps.send(tuple(self.value))
        except StopIteration:
            pass

    def result(self):
        for _ in range(3):
            self.step()
        return self.value[0]


class Cube:
    def __init__(self, axis, size):
        self.axis = axis
        self.size = size
        self.bits = [1 << bit for bit in range(size.bit_length() - 1)]

    def swap(self, value, mask):
        return lax.ppermute(value, self.axis, [(i, i ^ mask) for i in range(self.size)])

    def doubled(self, block):
        held = block[None]
        for bit in self.bits:
            held = jnp.concatenate([held, self.swap(held, bit)])
        order = jnp.arange(self.size, dtype=jnp.int32)
        here = lax.axis_index(self.axis)
        chosen = ((order[:, None] ^ order[None, :]) == here).astype(BF16)
        return dot(chosen, held.reshape(self.size, -1)).reshape((self.size,) + block.shape)

    def total(self, value):
        for bit in self.bits:
            value = value + self.swap(value, bit)
        return value


class Plane(Cube):
    def __init__(self, size):
        super().__init__("dp", size)
        self.chips = self.bits[1:]
        self.masks = [0]
        for mask in self.chips:
            self.masks = self.masks + [held ^ mask for held in self.masks]

    def gather_chips(self, block, chips):
        if not chips:
            return [(0, 0, block)]
        if len(chips) == 2:
            first, second = chips
            one = self.swap(block, first)
            two = self.swap(block, second)
            half = block.shape[0] // 2
            low = self.swap(one[:half], second)
            high = self.swap(two[half:], first)
            return [
                (0, 0, block),
                (first, 0, one),
                (second, 0, two),
                (first ^ second, 0, low),
                (first ^ second, half, high),
            ]
        held = self.gather_chips(block, chips[:-1])
        return held + [(m ^ chips[-1], at, self.swap(part, chips[-1])) for m, at, part in held]

    def pieces(self, block):
        held = self.gather_chips(block, self.chips)
        return held + [(m ^ 1, at, self.swap(part, 1)) for m, at, part in held]

    def scatter_chips(self, parts, chips):
        if not chips:
            return parts[0].astype(F32)
        count = len(parts) // 2
        far = [self.swap(part, chips[-1]) for part in parts[count:]]
        merged = [(a.astype(F32) + b).astype(BF16) for a, b in zip(parts[:count], far)]
        return self.scatter_chips(merged, chips[:-1])

    def scatter_steps(self, near, far):
        merged = (near.astype(F32) + self.swap(far, 1)).astype(BF16)
        (merged,) = yield (merged,)
        parts = jnp.split(merged, len(self.masks))
        if len(self.chips) != 2:
            result = self.scatter_chips(parts, self.chips)
            (result,) = yield (result,)
            yield (result,)
            return
        first, second = self.chips
        own, one, two, both = parts
        half = own.shape[0] // 2
        from_two = self.swap(both[:half], second).astype(F32)
        from_one = self.swap(both[half:], first).astype(F32)
        one = jnp.concatenate([one[:half] + from_two, one[half:].astype(F32)]).astype(BF16)
        two = jnp.concatenate([two[:half].astype(F32), two[half:] + from_one]).astype(BF16)
        one, two = yield (one, two)
        yield (own.astype(F32) + self.swap(one, first) + self.swap(two, second),)

    def collect(self, pieces, index=None):
        total = self.size * sum(part.shape[0] for m, _, part in pieces if m == 0)
        rows = total // self.size
        if index is None:
            order = self.masks + [mask ^ 1 for mask in self.masks]
            starts = jnp.array([order.index(m) * rows + at for m, at, _ in pieces], jnp.int32)
        else:
            blocks = jnp.array([m for m, _, _ in pieces], jnp.int32) ^ index
            starts = blocks * rows + jnp.array([at for _, at, _ in pieces], jnp.int32)
        arrays = [part for _, _, part in pieces]
        cols = arrays[0].shape[1]
        count = len(arrays)
        firsts = [0]
        for part in arrays:
            firsts.append(firsts[-1] + part.shape[0])

        def kernel(starts_ref, *refs):
            sources, out_ref, held, arrived, sent = refs[:count], *refs[count:]
            loads = []
            stores = []
            for i in range(count):
                length = arrays[i].shape[0]
                slot = held.at[pl.ds(firsts[i], length)]
                start = pl.multiple_of(starts_ref[i], 8)
                loads.append(pltpu.make_async_copy(sources[i], slot, arrived.at[i]))
                target = out_ref.at[pl.ds(start, length)]
                stores.append(pltpu.make_async_copy(slot, target, sent.at[i]))
            for load in loads:
                load.start()
            for load, store in zip(loads, stores):
                load.wait()
                store.start()
            for store in stores:
                store.wait()

        return pl.pallas_call(
            kernel,
            out_shape=jax.ShapeDtypeStruct((total, cols), arrays[0].dtype),
            in_specs=[pl.BlockSpec(memory_space=pltpu.SMEM)]
            + [pl.BlockSpec(memory_space=pl.ANY)] * count,
            out_specs=pl.BlockSpec(memory_space=pl.ANY),
            scratch_shapes=[
                pltpu.VMEM((total, cols), arrays[0].dtype),
                pltpu.SemaphoreType.DMA((count,)),
                pltpu.SemaphoreType.DMA((count,)),
            ],
            cost_estimate=pl.CostEstimate(
                flops=0, transcendentals=0, bytes_accessed=4 * total * cols
            ),
        )(starts, *arrays)

    def weight_grad(self, pairs, masks, index):
        width = pairs[0][0].shape[1] // self.size
        cols = pairs[0][1].shape[1]
        table = jnp.array(masks, jnp.int32) ^ index
        steps = len(masks) // 2
        count = len(pairs)

        def kernel(table_ref, *refs):
            lefts, rights, out_ref = refs[: 2 * count], refs[2 * count : 3 * count], refs[-1]
            for side in range(2):
                total = None
                for p in range(count):
                    part = dot(lefts[2 * p + side][...], rights[p][...], 0, 0)
                    total = part if total is None else total + part
                out_ref[pl.ds(side * width, width), :] = total.astype(BF16)

        specs = []
        operands = []
        for left, _ in pairs:
            rows = left.shape[0]
            specs.append(pl.BlockSpec((rows, width), lambda r, t: (0, t[2 * r])))
            specs.append(pl.BlockSpec((rows, width), lambda r, t: (0, t[2 * r + 1])))
            operands += [left, left]
        for _, right in pairs:
            specs.append(pl.BlockSpec(right.shape, lambda r, t: (0, 0)))
            operands.append(right)
        depth = sum(left.shape[0] for left, _ in pairs)
        return pl.pallas_call(
            kernel,
            out_shape=jax.ShapeDtypeStruct((len(masks) * width, cols), BF16),
            grid_spec=pltpu.PrefetchScalarGridSpec(
                num_scalar_prefetch=1,
                grid=(steps,),
                in_specs=specs,
                out_specs=pl.BlockSpec((2 * width, cols), lambda r, t: (r, 0)),
            ),
            cost_estimate=pl.CostEstimate(
                flops=2 * depth * len(masks) * width * cols,
                transcendentals=0,
                bytes_accessed=2 * (depth + len(masks) * width) * cols
                + 2 * depth * len(masks) * width,
            ),
        )(table, *operands)


def grid_call(kernel, grid, ins, outs, scratch=(), prefetch=(), flops=0, transcendentals=0):
    arrays = [array for array, _, _ in ins]
    results = [jax.ShapeDtypeStruct(shape, dtype) for shape, dtype, _, _ in outs]
    moved = sum(array.size * array.dtype.itemsize for array in arrays)
    moved += sum(result.size * jnp.dtype(result.dtype).itemsize for result in results)
    return pl.pallas_call(
        kernel,
        out_shape=results,
        grid_spec=pltpu.PrefetchScalarGridSpec(
            num_scalar_prefetch=len(prefetch),
            grid=grid,
            in_specs=[pl.BlockSpec(block, at) for _, block, at in ins],
            out_specs=[pl.BlockSpec(block, at) for _, _, block, at in outs],
            scratch_shapes=list(scratch),
        ),
        cost_estimate=pl.CostEstimate(
            flops=int(flops), transcendentals=int(transcendentals), bytes_accessed=int(moved)
        ),
    )(*prefetch, *arrays)


def decay_mask(log_decay, seg_col, seg_row):
    length = seg_col.shape[0]
    centre = length // 2
    down = lax.broadcasted_iota(jnp.int32, (length, 1), 0)
    along = lax.broadcasted_iota(jnp.int32, (1, length), 1)
    rows = jnp.exp((down - centre).astype(F32) * log_decay)
    cols = jnp.exp((centre - along).astype(F32) * log_decay)
    visible = (down >= along) & (seg_col == seg_row)
    return jnp.where(visible, rows * cols, 0.0)


def rotate(field, cosine, sine):
    half = field.shape[-1] // 2
    lower = field[:, :half]
    upper = field[:, half:]
    return jnp.concatenate([lower * cosine - upper * sine, upper * cosine + lower * sine], axis=-1)


def retain(x_full, gain, bias, segs, log_decays, tables, qk_full, vg_full, heads):
    length, width = x_full.shape
    seg_col, seg_row = segs
    chunk = min(128, length)

    def kernel(
        decay_ref, x_ref, gain_ref, bias_ref, col_ref, row_ref, cos_ref, sin_ref, wq, wk, wv, wg,
        normed_ref, mean_ref, inv_ref, q_ref, k_ref, v_ref, a_ref, gate_ref, on_ref, r_ref, gated_ref,
    ):
        head = pl.program_id(0)

        @pl.when(head == 0)
        def _():
            for first in range(0, length, chunk):
                rows = pl.ds(first, chunk)
                values = x_ref[rows, :].astype(F32)
                mean = jnp.mean(values, axis=-1, keepdims=True)
                centred = values - mean
                inv = lax.rsqrt(jnp.mean(centred * centred, axis=-1, keepdims=True) + EPS)
                normed_ref[rows, :] = (centred * inv * gain_ref[...] + bias_ref[...]).astype(BF16)
                mean_ref[rows, :] = mean
                inv_ref[rows, :] = inv

        normed = normed_ref[...]
        cosine = cos_ref[...]
        sine = sin_ref[...]
        q_head = rotate(dot(normed, wq[...]), cosine, sine).astype(BF16)
        k_head = (rotate(dot(normed, wk[...]), cosine, sine) * DK ** (-0.5)).astype(BF16)
        q_ref[...] = q_head
        k_ref[...] = k_head
        v_head = dot(normed, wv[...]).astype(BF16)
        v_ref[...] = v_head
        mask = decay_mask(decay_ref[head], col_ref[...], row_ref[...])
        weights = (dot(q_head, k_head, 1, 1) * mask).astype(BF16)
        a_ref[0] = weights
        out = dot(weights, v_head)
        mean = jnp.mean(out, axis=-1, keepdims=True)
        centred = out - mean
        inv = lax.rsqrt(jnp.mean(centred * centred, axis=-1, keepdims=True) + GROUP_EPS)
        grouped = centred * inv
        on_ref[...] = grouped.astype(BF16)
        r_ref[0] = inv
        gate = dot(normed, wg[...])
        gate_ref[...] = gate.astype(BF16)
        gated_ref[...] = (gate / (1.0 + jnp.exp(-gate)) * grouped).astype(BF16)

    whole = lambda h, t: (0, 0)
    one = lambda h, t: (0, h)
    return grid_call(
        kernel,
        (heads,),
        [
            (x_full, (length, width), whole),
            (gain, (1, width), whole),
            (bias, (1, width), whole),
            (seg_col, (length, 1), whole),
            (seg_row, (1, length), whole),
            (tables[0], (length, DK // 2), whole),
            (tables[1], (length, DK // 2), whole),
            (qk_full, (width, DK), one),
            (qk_full, (width, DK), lambda h, t: (0, heads + h)),
            (vg_full, (width, DV), one),
            (vg_full, (width, DV), lambda h, t: (0, heads + h)),
        ],
        [
            ((length, width), BF16, (length, width), whole),
            ((length, 1), F32, (length, 1), whole),
            ((length, 1), F32, (length, 1), whole),
            ((length, heads * DK), BF16, (length, DK), one),
            ((length, heads * DK), BF16, (length, DK), one),
            ((length, heads * DV), BF16, (length, DV), one),
            ((heads, length, length), BF16, (1, length, length), lambda h, t: (h, 0, 0)),
            ((length, heads * DV), BF16, (length, DV), one),
            ((length, heads * DV), BF16, (length, DV), one),
            ((heads, length, 1), F32, (1, length, 1), lambda h, t: (h, 0, 0)),
            ((length, heads * DV), BF16, (length, DV), one),
        ],
        prefetch=(log_decays,),
        flops=2 * length * heads * (2 * width * (DK + DV) + length * (DK + DV)),
        transcendentals=length * heads * DV,
    )


def retain_back(d_rows, out_full, segs, log_decays, tables, saved, heads):
    length, width = d_rows.shape
    seg_col, seg_row = segs
    q_all, k_all, v_all, a_all, gate_all, on_all, r_all = saved

    def kernel(
        decay_ref, d_ref, wo, col_ref, row_ref, cos_ref, sin_ref, q_ref, k_ref, v_ref, a_ref, gate_ref,
        on_ref, r_ref, d_qk_ref, d_vg_ref,
    ):
        head = pl.program_id(0)
        d_gated = dot(d_ref[...], wo[...])
        gate = gate_ref[...].astype(F32)
        grouped = on_ref[...].astype(F32)
        sig = 1.0 / (1.0 + jnp.exp(-gate))
        d_gate = d_gated * grouped * sig * (1.0 + gate * (1.0 - sig))
        at = pl.multiple_of((heads + head) * DV, DV)
        d_vg_ref[:, pl.ds(at, DV)] = d_gate.astype(BF16)
        d_out = norm_back(d_gated * (gate * sig), 1.0, grouped, r_ref[0]).astype(BF16)
        mask = decay_mask(decay_ref[head], col_ref[...], row_ref[...])
        d_weights = (dot(d_out, v_ref[...], 1, 1) * mask).astype(BF16)
        at = pl.multiple_of(head * DV, DV)
        d_vg_ref[:, pl.ds(at, DV)] = dot(a_ref[0], d_out, 0, 0).astype(BF16)
        cosine = cos_ref[...]
        sine = -sin_ref[...]
        at = pl.multiple_of(head * DK, DK)
        d_qk_ref[:, pl.ds(at, DK)] = rotate(dot(d_weights, k_ref[...]), cosine, sine).astype(BF16)
        at = pl.multiple_of((heads + head) * DK, DK)
        d_key = rotate(dot(d_weights, q_ref[...], 0, 0), cosine, sine) * DK ** (-0.5)
        d_qk_ref[:, pl.ds(at, DK)] = d_key.astype(BF16)

    whole = lambda h, t: (0, 0)
    one = lambda h, t: (0, h)
    return grid_call(
        kernel,
        (heads,),
        [
            (d_rows, (length, width), whole),
            (out_full, (width, DV), one),
            (seg_col, (length, 1), whole),
            (seg_row, (1, length), whole),
            (tables[0], (length, DK // 2), whole),
            (tables[1], (length, DK // 2), whole),
            (q_all, (length, DK), one),
            (k_all, (length, DK), one),
            (v_all, (length, DV), one),
            (a_all, (1, length, length), lambda h, t: (h, 0, 0)),
            (gate_all, (length, DV), one),
            (on_all, (length, DV), one),
            (r_all, (1, length, 1), lambda h, t: (h, 0, 0)),
        ],
        [
            ((length, 2 * heads * DK), BF16, (length, 2 * heads * DK), whole),
            ((length, 2 * heads * DV), BF16, (length, 2 * heads * DV), whole),
        ],
        prefetch=(log_decays,),
        flops=2 * length * heads * (width * DV + length * (2 * DK + 2 * DV)),
        transcendentals=length * heads * DV,
    )


def project_back(d_qk, d_vg, qk_full, vg_full, x_full, mean, inv):
    length = d_qk.shape[0]
    width = qk_full.shape[0]
    tile = min(512, width)

    def kernel(d_qk_ref, d_vg_ref, wqk, wvg, x_ref, mean_ref, inv_ref, out_ref, sums_ref):
        total = dot(d_qk_ref[...], wqk[...], 1, 1) + dot(d_vg_ref[...], wvg[...], 1, 1)
        out_ref[...] = total.astype(BF16)
        scaled = (x_ref[...].astype(F32) - mean_ref[...]) * inv_ref[...]
        sums_ref[0:1, :] = jnp.sum(total * scaled, axis=0, keepdims=True)
        sums_ref[1:2, :] = jnp.sum(total, axis=0, keepdims=True)

    whole = lambda j: (0, 0)
    down = lambda j: (j, 0)
    along = lambda j: (0, j)
    depth = d_qk.shape[1] + d_vg.shape[1]
    return grid_call(
        kernel,
        (width // tile,),
        [
            (d_qk, d_qk.shape, whole),
            (d_vg, d_vg.shape, whole),
            (qk_full, (tile, d_qk.shape[1]), down),
            (vg_full, (tile, d_vg.shape[1]), down),
            (x_full, (length, tile), along),
            (mean, (length, 1), whole),
            (inv, (length, 1), whole),
        ],
        [
            ((length, width), BF16, (length, tile), along),
            ((2, width), F32, (2, tile), along),
        ],
        flops=2 * length * width * depth,
    )


def ffn_forward_back(pieces_two, pieces_dy, up_full, down_full):
    width, hidden = up_full.shape
    sizes = [part.shape[0] for part in pieces_two]
    count = len(sizes)
    total = sum(sizes)
    tile = min(512, total)
    spots = []
    for which in range(2):
        first = 0
        for size in sizes:
            spots.append((which, first, size))
            first += size

    def kernel(*refs):
        sources = refs[: 2 * count]
        up_ref, down_ref, two_ref, dy_ref, hidden_ref, d_up_ref, term_ref, two, dy, arrived, sent = refs[
            2 * count :
        ]
        held = (two, dy)
        loads = []
        for i, (which, first, size) in enumerate(spots):
            slot = held[which].at[pl.ds(first, size)]
            loads.append(pltpu.make_async_copy(sources[i], slot, arrived.at[i]))
        for load in loads:
            load.start()
        for load in loads:
            load.wait()
        stores = [
            pltpu.make_async_copy(two, two_ref, sent.at[0]),
            pltpu.make_async_copy(dy, dy_ref, sent.at[1]),
        ]
        for store in stores:
            store.start()
        for first in range(0, total, tile):
            rows = pl.ds(first, tile)
            up = dot(two[rows, :], up_ref[...])
            d_hidden = dot(dy[rows, :], down_ref[...])
            cdf = 0.5 * (1.0 + lax.erf(up * ROOT_HALF))
            hidden_ref[rows, :] = (up * cdf).astype(BF16)
            slope = cdf + up * jnp.exp(-0.5 * up * up) * INV_ROOT_TWO_PI
            d_up = (d_hidden * slope).astype(BF16)
            d_up_ref[rows, :] = d_up
            term_ref[rows, :] = dot(d_up, up_ref[...], 1, 1).astype(BF16)
        for store in stores:
            store.wait()

    vmem = pl.BlockSpec(memory_space=pltpu.VMEM)
    hbm = pl.BlockSpec(memory_space=pl.ANY)
    return pl.pallas_call(
        kernel,
        out_shape=[
            jax.ShapeDtypeStruct((total, width), BF16),
            jax.ShapeDtypeStruct((total, width), BF16),
            jax.ShapeDtypeStruct((total, hidden), BF16),
            jax.ShapeDtypeStruct((total, hidden), BF16),
            jax.ShapeDtypeStruct((total, width), BF16),
        ],
        in_specs=[hbm] * (2 * count) + [vmem, vmem],
        out_specs=[hbm, hbm, vmem, vmem, vmem],
        scratch_shapes=[
            pltpu.VMEM((total, width), BF16),
            pltpu.VMEM((total, width), BF16),
            pltpu.SemaphoreType.DMA((2 * count,)),
            pltpu.SemaphoreType.DMA((2,)),
        ],
        cost_estimate=pl.CostEstimate(
            flops=6 * total * width * hidden,
            transcendentals=2 * total * hidden,
            bytes_accessed=10 * total * width + 4 * width * hidden,
        ),
    )(*pieces_two, *pieces_dy, up_full, down_full)


def ffn_weight_grad(pairs_up, pairs_down, slots):
    width = pairs_up[0][0].shape[1]
    hidden = pairs_up[0][1].shape[1]
    share = hidden // slots
    tile = min(512, width)
    count = len(pairs_up)

    def kernel(*refs):
        outs = refs[4 * count :]
        for which in range(2):
            total = None
            for p in range(count):
                left = refs[2 * which * count + 2 * p]
                right = refs[2 * which * count + 2 * p + 1]
                part = dot(left[...], right[...], 0, 0)
                total = part if total is None else total + part
            for slot in range(slots):
                outs[0][slot, :, which * share : (which + 1) * share] = total[
                    :, slot * share : (slot + 1) * share
                ].astype(BF16)

    specs = []
    operands = []
    for left, right in list(pairs_up) + list(pairs_down):
        specs.append(pl.BlockSpec((left.shape[0], tile), lambda r: (0, r)))
        specs.append(pl.BlockSpec(right.shape, lambda r: (0, 0)))
        operands += [left, right]
    depth = sum(left.shape[0] for left, _ in pairs_up)
    return pl.pallas_call(
        kernel,
        out_shape=jax.ShapeDtypeStruct((slots, width, 2 * share), BF16),
        grid=(width // tile,),
        in_specs=specs,
        out_specs=pl.BlockSpec((slots, tile, 2 * share), lambda r: (0, r, 0)),
        cost_estimate=pl.CostEstimate(
            flops=4 * depth * width * hidden,
            transcendentals=0,
            bytes_accessed=4 * (depth * width + depth * hidden + width * hidden),
        ),
    )(*operands)


def body(
    dp_size,
    mp_size,
    tokens,
    segments,
    query_weight,
    key_weight,
    value_weight,
    gate_weight,
    out_weight,
    up_weight,
    down_weight,
    gain_before,
    bias_before,
    gain_middle,
    bias_middle,
    cotangent,
):
    plane = Plane(dp_size)
    line = Cube("mp", mp_size)
    index = lax.axis_index("dp")
    micro_count, seq_count, local_length, width = tokens.shape
    heads = query_weight.shape[1] // DK
    hidden_share = up_weight.shape[1] // dp_size
    hidden_here = mp_size * hidden_share
    length = mp_size * local_length
    share = gain_before.shape[0]
    count = micro_count * seq_count
    items = range(count)
    tokens_own = tokens.reshape(count, local_length, width)

    qk_pieces = plane.pieces(jnp.concatenate([query_weight, key_weight], axis=1))
    vg_pieces = plane.pieces(jnp.concatenate([value_weight, gate_weight], axis=1))
    norm_stack = plane.doubled(jnp.stack([gain_before, bias_before, gain_middle, bias_middle]))
    seg_full = line.doubled(segments.reshape(count, local_length).astype(BF16))
    ffn_share = jnp.concatenate(
        [
            up_weight.reshape(-1, dp_size, hidden_share),
            down_weight.reshape(-1, dp_size, hidden_share),
        ],
        axis=2,
    ).reshape(-1, 2 * dp_size * hidden_share)
    near_vg = [part for _, _, part in vg_pieces[1:3]]
    norm_stack, seg_full, later, ffn_share, *near_vg = tie(
        norm_stack, seg_full, tokens_own[1:], ffn_share, *near_vg
    )
    vg_pieces[1:3] = [(m, at, new) for (m, at, _), new in zip(vg_pieces[1:3], near_vg)]
    ffn_share = lax.all_to_all(ffn_share, "dp", 1, 0, tiled=True)
    tokens_full = [
        lax.all_gather(part, "mp", axis=0, tiled=True)
        for part in [tokens_own[0]] + [later[i] for i in range(count - 1)]
    ]
    out_pieces = plane.pieces(out_weight)
    qk_full, vg_full, out_full = [
        plane.collect(pieces, index) for pieces in (qk_pieces, vg_pieces, out_pieces)
    ]
    norm_stack = norm_stack.transpose(1, 0, 2).reshape(4, width)
    gain_one, bias_one, gain_two, bias_two = [norm_stack[i : i + 1] for i in range(4)]
    seg_full = seg_full.transpose(1, 0, 2).reshape(count, length)
    segs = [(seg_full[i][:, None], seg_full[i][None, :]) for i in items]
    head_ids = lax.axis_index("mp") * heads + jnp.arange(heads, dtype=jnp.int32)
    log_decays = jnp.log(1.0 - 2.0 ** (-5.0 - head_ids.astype(F32)))
    tables = rotary_tables(length, DK)
    x_own = tokens_own.reshape(count * local_length, width).astype(F32)
    dy_own = cotangent.reshape(count * local_length, width)

    kept = []
    mixes = []
    for i in items:
        x_full = tokens_full[i]
        normed, mean, inv, *saved, gated = retain(
            x_full, gain_one, bias_one, segs[i], log_decays, tables, qk_full, vg_full, heads
        )
        kept.append((x_full, normed, mean, inv, saved, gated))
        mixed = dot(gated, out_full, 1, 1).astype(BF16)
        if i + 1 < count:
            mixed, tokens_full[i + 1] = tie(mixed, tokens_full[i + 1])
        mixes.append(lax.psum_scatter(mixed, "mp", scatter_dimension=0, tiled=True))
    ffn_share, mixed = tie(ffn_share, mixed)
    ffn_all = lax.all_gather(ffn_share, "mp", axis=0)
    up_full = ffn_all[:, :, :hidden_share].transpose(1, 0, 2).reshape(width, hidden_here)
    down_full = ffn_all[:, :, hidden_share:].transpose(1, 0, 2).reshape(width, hidden_here)

    dy_pieces = [part for _, _, part in plane.pieces(dy_own)]
    mix = jnp.concatenate(mixes).astype(F32)
    resid = x_own + mix
    norm_two, scaled_two, inv_two = layer_norm(resid, gain_two, bias_two)
    two_pieces = [part for _, _, part in plane.pieces(norm_two.astype(BF16))]
    half = len(two_pieces) // 2
    far = ffn_forward_back(two_pieces[half:], dy_pieces[half:], up_full, down_full)
    tied = tie(*far, *two_pieces[:half])
    far, two_pieces[:half] = tied[: len(far)], tied[len(far) :]
    near = ffn_forward_back(two_pieces[:half], dy_pieces[:half], up_full, down_full)
    staged = Staged(plane.scatter_steps(near[4], far[4]))
    sides = []
    for side in (near, far):
        two, dy, hidden, d_up = side[:4]
        sides.append([two, dy, hidden, d_up])
    sides[0][3], sides[1][3] = staged.ahead_of(sides[0][3], sides[1][3])
    ffn_parts = ffn_weight_grad(
        [(two, d_up) for two, _, _, d_up in sides],
        [(dy, hidden) for _, dy, hidden, _ in sides],
        mp_size,
    )
    ffn_parts, sides[0][2], sides[1][2] = staged.ahead_of(ffn_parts, sides[0][2], sides[1][2])
    ffn_grad = lax.psum_scatter(ffn_parts, "mp", scatter_dimension=0, tiled=False)
    d_normtwo = staged.result()
    d_resid = dy_own.astype(F32) + norm_back(d_normtwo, gain_two, scaled_two, inv_two)
    d_own = d_resid.astype(BF16)
    d_own, ffn_grad = tie(d_own, ffn_grad)
    d_full = [
        lax.all_gather(d_own[i * local_length : (i + 1) * local_length], "mp", axis=0, tiled=True)
        for i in items
    ]
    term_far = dot(sides[1][2], down_full, 1, 1).astype(BF16)
    term_near = dot(sides[0][2], down_full, 1, 1).astype(BF16)
    staged_out = Staged(plane.scatter_steps(term_near, term_far))

    sums = 0.0
    backs = []
    d_normones = []
    for i in items:
        x_full, normed, mean, inv, saved, gated = kept[i]
        d_qk, d_vg = retain_back(d_full[i], out_full, segs[i], log_decays, tables, saved, heads)
        before, new_sums = project_back(d_qk, d_vg, qk_full, vg_full, x_full, mean, inv)
        sums = sums + new_sums
        if i + 1 < count:
            before, out_full = tie(before, out_full)
        elif i:
            d_normones[-1], before = tie(d_normones[-1], before)
        before, d_qk, d_vg = tie(before, d_qk, d_vg)
        backs.append((d_qk, d_vg))
        d_normones.append(lax.psum_scatter(before, "mp", scatter_dimension=0, tiled=True))
    block_out = resid + staged_out.result()
    d_normone = jnp.concatenate(d_normones).astype(F32)
    _, scaled_one, inv_one = layer_norm(x_own, gain_one, bias_one)
    tokens_grad = d_resid + norm_back(d_normone, gain_one, scaled_one, inv_one)

    near_masks = plane.masks
    far_masks = [mask ^ 1 for mask in near_masks]
    groups = [
        [(d_full[i], kept[i][5]) for i in items],
        [(kept[i][1], backs[i][1]) for i in items],
        [(kept[i][1], backs[i][0]) for i in items],
    ]
    staged = []
    for pairs in groups:
        if staged:
            rights = staged[-1].ahead_of(*[right for _, right in pairs])
            pairs = [(left, right) for (left, _), right in zip(pairs, rights)]
        far_part = plane.weight_grad(pairs, far_masks, index)
        if staged:
            rights = staged[-1].ahead_of(*[right for _, right in pairs])
            pairs = [(left, right) for (left, _), right in zip(pairs, rights)]
        far_part, *rights = tie(far_part, *[right for _, right in pairs])
        pairs = [(left, right) for (left, _), right in zip(pairs, rights)]
        near_part = plane.weight_grad(pairs, near_masks, index)
        staged.append(Staged(plane.scatter_steps(near_part, far_part)))
    out_grad, vg_grad, qk_grad = [stage.result() for stage in staged]
    sums = jnp.concatenate(
        [
            sums,
            jnp.sum(d_normtwo * scaled_two, axis=0, keepdims=True),
            jnp.sum(d_normtwo, axis=0, keepdims=True),
        ]
    )
    sums = line.total(plane.total(sums))
    norm_grads = lax.dynamic_slice_in_dim(sums, index * share, share, axis=1)
    ffn_grad = lax.all_to_all(ffn_grad, "dp", 0, 1, tiled=True)
    ffn_grad = ffn_grad.reshape(-1, dp_size, 2, hidden_share).astype(F32)
    up_grad = ffn_grad[:, :, 0].reshape(-1, dp_size * hidden_share)
    down_grad = ffn_grad[:, :, 1].reshape(-1, dp_size * hidden_share)

    shape = (micro_count, seq_count, local_length, width)
    return (
        block_out.astype(BF16).reshape(shape),
        tokens_grad.astype(BF16).reshape(shape),
        qk_grad[:, : heads * DK],
        qk_grad[:, heads * DK :],
        vg_grad[:, : heads * DV],
        vg_grad[:, heads * DV :],
        out_grad,
        up_grad,
        down_grad,
        norm_grads,
    )


def solution(mesh):
    rows = P(None, "dp", "mp", None)
    weight = P("dp", "mp")
    vector = P("dp")
    in_specs = (rows, P(None, "dp", "mp")) + (weight,) * 7 + (vector,) * 4 + (rows,)
    out_specs = (rows, rows) + (weight,) * 7 + (P(None, "dp"),)
    return jax.shard_map(
        functools.partial(body, mesh.shape["dp"], mesh.shape["mp"]),
        mesh=mesh,
        in_specs=in_specs,
        out_specs=out_specs,
        check_vma=False,
    )
```
